32 devices in a mesh: ctx: 8 (over z, x), head: 4 (over y, core).
Axes of the slice: x: 2, y: 2, z: 4, core: 2. Of those that a mesh axis runs over, the one named last changes fastest.
Arguments:
- probe_vectors: bfloat16 [1024, 8192], P('ctx', 'head'), may hold values from -160 to 160
- lookup_tensor: bfloat16 [8192, 1024], P('ctx', 'head'), may hold values from -4.5 to 4.5
- payload_tensor: bfloat16 [8192, 1024], P('ctx', 'head'), may hold values from -6 to 6
- sequence_locations: int32 [1024], replicated, may hold values from 0 to 8191, as said below
- attention_return_matrix: bfloat16 [8192, 8192], P('head', 'ctx'), may hold values from -0.0625 to 0.0625
- skip_stream_state: bfloat16 [1024, 8192], P('head', 'ctx'), may hold values from -4 to 4
- early_rescaling_factor: float32 [8192], P('ctx'), may hold values from 0.5 to 1.5
- lexicon_projection_matrix: bfloat16 [8192, 65536], P(None, ('ctx', 'head')), may hold values from -0.1875 to 0.1875
- calibrating_divisor: float32 [1024], replicated, may hold values from 0.02 to 1
- desired_tokens_list: int32 [1024], replicated, may hold values from 0 to 65535
Outputs:
- hidden: bfloat16 [1024, 8192], P('head', 'ctx')
- logprob: float32 [1024], replicated
The draws below stay inside these ranges and needn't reach their ends.
Inputs may be any that keep to these rules, and one draw needn't show every extreme that they name: `sequence_locations`: query i stands at a position from i * 8 to (i + 1) * 8 - 1; the last query stands at 8191.
All inputs are finite; a program needn't handle non-finite values.
Results may differ from the reference program's by a relative error of at most 0.0014.
The reference program's roundings to bfloat16 on the way count: a program that leaves them out, or rounds other values in their place, can miss the bound.
Values may be sent and summed in bfloat16 or wider, within the bound.
No kernel may reach another device: no remote copies, remote signals or barrier semaphores. Data moves between devices by JAX's collectives and lax.ppermute only.
A program may use at most 192 MiB of HBM per device.

```python
import math
import jax
import jax.numpy as jnp
import numpy as np
from jax import lax

D = 8192
QUERY_HEAD_COUNT = 64
KEY_VALUE_HEADS = 8
HEAD_SIZE = 128
V = 65536
EXIT_QUERIES = 1024
CONTEXT_PER_PART = 1024
CONTEXT_TOTAL = 8192


def position_draw(key):
    span = CONTEXT_TOTAL // EXIT_QUERIES
    offsets = jax.random.randint(jax.random.fold_in(key, 3), (EXIT_QUERIES,), 0, span)
    row_ids = jnp.arange(EXIT_QUERIES, dtype=jnp.int32)
    offsets = jnp.where(row_ids == EXIT_QUERIES - 1, 0, offsets)
    return ((row_ids + 1) * span - 1 - offsets).astype(jnp.int32)


def attention_draw(key):
    base_offset = jax.random.fold_in(key, 11)
    query_vals = 2.5 * jax.random.normal(jax.random.fold_in(base_offset, 1), (EXIT_QUERIES, QUERY_HEAD_COUNT * HEAD_SIZE), jnp.float32)
    query_vals = jnp.clip(query_vals, -12.0, 12.0)
    key_entries = jax.random.normal(jax.random.fold_in(base_offset, 2), (CONTEXT_TOTAL, KEY_VALUE_HEADS * HEAD_SIZE), jnp.float32)
    key_entries = jnp.clip(key_entries, -4.5, 4.5)
    return (query_vals, key_entries)


def draw_sequence_locations(key, part):
    return position_draw(key)


def draw_probe_vectors(key, part):
    return attention_draw(key)[0].astype(jnp.bfloat16)


def draw_lookup_tensor(key, part):
    return attention_draw(key)[1].astype(jnp.bfloat16)


def draw_calibrating_divisor(key, part):
    base_offset = jax.random.fold_in(key, 23)
    spread = jax.random.uniform(base_offset, (EXIT_QUERIES,), jnp.float32)
    temps = 0.25 * 4.0 ** spread
    return temps


def place_ends(drawn, own_key, smallest, high):
    longest = drawn.shape.index(max(drawn.shape))
    spots = []
    for shift in (0, 1):
        where = [jax.random.randint(jax.random.fold_in(own_key, axis), (), 0, length) for axis, length in enumerate(drawn.shape)]
        where[longest] = (where[longest] + shift) % drawn.shape[longest]
        spots.append(tuple(where))
    return drawn.at[spots[0]].set(smallest).at[spots[1]].set(high)


def block_levels(stream_key, extent, cuts, least, largest):
    gain, own = 1.0, jax.random.fold_in(stream_key, 6)
    for axis_at, blocks in cuts:
        heights = jnp.exp(jax.random.uniform(jax.random.fold_in(own, axis_at), (blocks,), jnp.float32, least / len(cuts), largest / len(cuts)))
        gain = gain * jnp.repeat(heights, extent[axis_at] // blocks).reshape([-1 if axis == axis_at else 1 for axis in range(len(extent))])
    return gain


def rank_table(count, lean):
    portions = [(1 << 20) // math.isqrt(standing ** lean) + 1 for standing in range(1, count + 1)]
    width = 1 + sum(portions) // (1 << 30)
    return np.cumsum(np.array([max(1, weight // width) for weight in portions]))


def ranked(own_key, extent, amount, lean):
    grid = rank_table(amount, lean)
    pick = jax.random.randint(jax.random.fold_in(own_key, 1), extent, 0, int(grid[amount - 1]))
    standing = jnp.searchsorted(jnp.asarray(grid, jnp.int32), pick, side="right")
    return jax.random.permutation(jax.random.fold_in(own_key, 2), amount)[standing].astype(jnp.int32)


def noise(stream_key, dims, scale, reach, split=(), held_as=jnp.bfloat16):
    level = block_levels(stream_key, dims, split, -0.22, 0.18) if split else 1.0
    result = jax.random.normal(stream_key, dims, jnp.float32) * scale * level
    return jnp.minimum(jnp.maximum(result, -reach), reach).astype(held_as)


def setup_inputs(seed: int = 0) -> dict:
    streams_of = jax.random.split(jax.random.key(seed), 11)
    probe_vectors = draw_probe_vectors(jax.random.fold_in(streams_of[10], 71), 0)
    lookup_tensor = draw_lookup_tensor(jax.random.fold_in(streams_of[10], 71), 0)
    payload_tensor = noise(streams_of[2], (CONTEXT_TOTAL, KEY_VALUE_HEADS * HEAD_SIZE), 1.0, 6.0, ((0, 8), (1, 4)))
    sequence_locations = draw_sequence_locations(jax.random.fold_in(streams_of[10], 71), 0)
    attention_return_matrix = noise(streams_of[4], (QUERY_HEAD_COUNT * HEAD_SIZE, D), (QUERY_HEAD_COUNT * HEAD_SIZE) ** -0.5, 0.0625, ((0, 4), (1, 8)))
    skip_stream_state = noise(streams_of[5], (EXIT_QUERIES, D), 0.3, 4.0, ((0, 4), (1, 8)))
    early_rescaling_factor = jnp.clip(1.0 + 0.1 * jax.random.normal(streams_of[6], (D,), jnp.float32), 0.5, 1.5)
    lexicon_projection_matrix = noise(streams_of[7], (D, V), (D // 9) ** -0.5, 0.1875, ((1, 32),))
    calibrating_divisor = draw_calibrating_divisor(jax.random.fold_in(streams_of[10], 71), 0)
    desired_tokens_list = place_ends(ranked(streams_of[9], (EXIT_QUERIES,), V, 2), jax.random.fold_in(streams_of[9], 3), 0, V - 1).astype(jnp.int32)
    return {"probe_vectors": probe_vectors, "lookup_tensor": lookup_tensor, "payload_tensor": payload_tensor, "sequence_locations": sequence_locations, "attention_return_matrix": attention_return_matrix, "skip_stream_state": skip_stream_state, "early_rescaling_factor": early_rescaling_factor, "lexicon_projection_matrix": lexicon_projection_matrix, "calibrating_divisor": calibrating_divisor, "desired_tokens_list": desired_tokens_list}


neg_big = -1e+30
eps = 1e-05

def head_attention(inputs, sequence_locations):
    query_head, key_head, value_head = inputs
    group_size = query_head.shape[1]
    scale_factor = HEAD_SIZE ** (-0.5)
    number_blocks = key_head.shape[0]
    start = (jnp.full((EXIT_QUERIES, group_size), neg_big, jnp.float32), jnp.zeros((EXIT_QUERIES, group_size), jnp.float32), jnp.zeros((EXIT_QUERIES, group_size, HEAD_SIZE), jnp.float32))

    def one_block(carry, block_inputs):
        run_max, run_sum, run_acc = carry
        key_block, value_block, block_index = block_inputs
        key_pos = block_index * CONTEXT_PER_PART + jnp.arange(CONTEXT_PER_PART, dtype=jnp.int32)
        scores = jnp.einsum('qhd,kd->qhk', query_head, key_block.astype(jnp.float32), precision=lax.Precision.HIGHEST) * scale_factor
        visible = key_pos[None, None, :] <= sequence_locations[:, None, None]
        block_max = lax.optimization_barrier(jnp.max(jnp.where(visible, scores, neg_big), axis=-1))
        weights = jnp.where(visible, jnp.exp(scores - block_max[..., None]), 0.0)
        block_sum = lax.optimization_barrier(jnp.sum(weights, axis=-1))
        rounded = lax.optimization_barrier(weights.astype(jnp.bfloat16)).astype(jnp.float32)
        block_acc = jnp.einsum('qhk,kd->qhd', rounded, value_block.astype(jnp.float32), precision=lax.Precision.HIGHEST)
        new_max = jnp.maximum(run_max, block_max)
        old_scale = jnp.exp(run_max - new_max)
        new_scale = jnp.exp(block_max - new_max)
        next_sum = run_sum * old_scale + block_sum * new_scale
        next_acc = run_acc * old_scale[..., None] + block_acc * new_scale[..., None]
        return ((new_max, next_sum, next_acc), None)
    block_ids = jnp.arange(number_blocks, dtype=jnp.int32)
    final, unused = lax.scan(one_block, start, (key_head, value_head, block_ids))
    return final[2] / final[1][..., None]

def reference(probe_vectors, lookup_tensor, payload_tensor, sequence_locations, attention_return_matrix, skip_stream_state, early_rescaling_factor, lexicon_projection_matrix, calibrating_divisor, desired_tokens_list):
    group_size = QUERY_HEAD_COUNT // KEY_VALUE_HEADS
    number_blocks = CONTEXT_TOTAL // CONTEXT_PER_PART
    every_query = probe_vectors.astype(jnp.float32).reshape(EXIT_QUERIES, KEY_VALUE_HEADS, group_size, HEAD_SIZE).transpose(1, 0, 2, 3)
    every_key = lookup_tensor.reshape(number_blocks, CONTEXT_PER_PART, KEY_VALUE_HEADS, HEAD_SIZE).transpose(2, 0, 1, 3)
    every_value = payload_tensor.reshape(number_blocks, CONTEXT_PER_PART, KEY_VALUE_HEADS, HEAD_SIZE).transpose(2, 0, 1, 3)
    heads_out = lax.map(lambda inputs: head_attention(inputs, sequence_locations), (every_query, every_key, every_value))
    attn = heads_out.transpose(1, 0, 2, 3).reshape(EXIT_QUERIES, QUERY_HEAD_COUNT * HEAD_SIZE).astype(jnp.bfloat16)
    mixed = jnp.dot(attn, attention_return_matrix, preferred_element_type=jnp.float32)
    hidden = (skip_stream_state.astype(jnp.float32) + mixed).astype(jnp.bfloat16)
    wide = hidden.astype(jnp.float32)
    mean_sq = lax.optimization_barrier(jnp.sum(wide * wide, axis=1)) / D
    normed = (wide * lax.rsqrt(mean_sq + eps)[:, None] * early_rescaling_factor[None, :]).astype(jnp.bfloat16)
    early_class_energies = jnp.dot(normed, lexicon_projection_matrix, preferred_element_type=jnp.float32)
    tempered_affinities = early_class_energies / calibrating_divisor[:, None]
    peak = lax.optimization_barrier(jnp.max(tempered_affinities, axis=1))
    total = lax.optimization_barrier(jnp.sum(jnp.exp(tempered_affinities - peak[:, None]), axis=1))
    picked = jnp.take_along_axis(tempered_affinities, desired_tokens_list[:, None].astype(jnp.int32), axis=1)[:, 0]
    logprob = picked - peak - jnp.log(total)
    return (hidden, logprob)
```

```python
import functools
import math

import jax
import jax.numpy as jnp
import numpy as np
from jax import lax
from jax.experimental import pallas as pl
from jax.experimental.pallas import tpu as pltpu
from jax.sharding import PartitionSpec as P

QUERY_HEAD_COUNT = 64
KEY_VALUE_HEADS = 8
HEAD_SIZE = 128

neg_big = -1e30
eps = 1e-05
AXES = ("ctx", "head")


class Moves:
    def __init__(self, mesh):
        self.ctx, self.head = mesh.shape["ctx"], mesh.shape["head"]

    def perm(self, ctx_to=None, head_to=None):
        pairs = []
        for i in range(self.ctx):
            for h in range(self.head):
                i2 = i if ctx_to is None else ctx_to(i)
                h2 = h if head_to is None else head_to(h)
                if i2 is not None and h2 is not None:
                    pairs.append((i * self.head + h, i2 * self.head + h2))
        return pairs

    def ctx_move(self, value, ctx_to):
        return lax.ppermute(value, AXES, self.perm(ctx_to=ctx_to))

    def head_move(self, value, head_to):
        return lax.ppermute(value, AXES, self.perm(head_to=head_to))

    def minor_swap(self, value):
        return self.ctx_move(value, lambda i: i ^ 1)

    def y_swap(self, value):
        return self.head_move(value, lambda h: h ^ 2)

    def core_swap(self, value):
        return self.head_move(value, lambda h: h ^ 1)


def ring_order(count):
    return list(range(0, count, 2)) + list(range(count - 1, 0, -2))


def ring_gather(moves, block, count, ahead, behind):
    order = ring_order(count)
    place = {v: p for p, v in enumerate(order)}

    def shifted(i, step):
        base = i // count * count
        return base + order[(place[i - base] + step) % count]

    def source(step):
        return np.array([shifted(i, step) for i in range(moves.ctx)], np.int32)

    found = [(source(0), block)]
    forward = backward = block
    for k in range(1, max(ahead, behind) + 1):
        if k <= ahead:
            forward = moves.ctx_move(forward, lambda i: shifted(i, 1))
            found.append((source(-k), forward))
        if k <= behind:
            backward = moves.ctx_move(backward, lambda i: shifted(i, -1))
            found.append((source(k), backward))
    return found


def line_slots(length):
    arrivals = []
    for z in range(length):
        mine = []
        for k in range(1, length):
            pair = []
            if z + k < length:
                pair.append(("down", k, z + k))
            if z - k >= 0:
                pair.append(("up", k, z - k))
            if z >= length // 2:
                pair.reverse()
            mine += pair
        arrivals.append(mine)
    return [[arrivals[z][s] for z in range(length)] for s in range(length - 1)]


def line_gather(moves, block, z):
    length = moves.ctx // 2
    got = {("up", 0): block, ("down", 0): block}
    for k in range(1, length):
        got["up", k] = moves.ctx_move(
            got["up", k - 1], lambda i: i + 2 if k - 1 <= i // 2 < length - 1 else None
        )
        got["down", k] = moves.ctx_move(
            got["down", k - 1], lambda i: i - 2 if 0 < i // 2 <= length - k else None
        )
    blocks, places = [block], [np.arange(length, dtype=np.int32)]
    for slot in line_slots(length):
        choices = {}
        for place, (way, k, _) in enumerate(slot):
            choices.setdefault((way, k), []).append(place)
        value = None
        for key, where_z in choices.items():
            if value is None:
                value = got[key]
            else:
                here = functools.reduce(jnp.logical_or, [z == p for p in where_z])
                value = jnp.where(here, got[key], value)
        blocks.append(value)
        places.append(np.array([entry[2] for entry in slot], np.int32))
    return blocks, places


def butterfly(moves, value, merge):
    step = 1
    while step < moves.head:
        value = merge(value, moves.head_move(value, lambda h: h ^ step))
        step *= 2
    step = 1
    while step < moves.ctx:
        value = merge(value, moves.ctx_move(value, lambda i: i ^ step))
        step *= 2
    return value


def attention_kernel(count, heads, table, loc_ref, q_ref, *rest):
    sources, (o_ref, k_buf, v_buf, sems) = rest[:count], rest[count:]
    block = pl.program_id(0)
    span = k_buf.shape[1]
    rows = q_ref.shape[1]
    factor = HEAD_SIZE ** (-0.5) * math.log2(math.e)

    @pl.when(block == 0)
    def _():
        copies = []
        for n, source in enumerate(sources):
            for part, buf in enumerate((k_buf, v_buf)):
                copies.append(
                    pltpu.make_async_copy(source.at[part], buf.at[table[n]], sems.at[n, part])
                )
        for copy in copies:
            copy.start()
        for copy in copies:
            copy.wait()

    query = jnp.concatenate(
        [q_ref[0, :, n * HEAD_SIZE : (n + 1) * HEAD_SIZE] for n in range(heads)], axis=0
    )

    def attend(j, carry, masked):
        run_max, run_sum, run_acc = carry
        scores = lax.dot_general(
            query, k_buf[j], (((1,), (1,)), ((), ())), preferred_element_type=jnp.float32
        )
        if masked:
            row_pos = jnp.concatenate([loc_ref[0]] * heads, axis=0)
            key_pos = j * span + lax.broadcasted_iota(jnp.int32, scores.shape, 1)
            scores = jnp.where(key_pos <= row_pos, scores, neg_big)
        block_max = jnp.max(scores, axis=1, keepdims=True)
        weights = jnp.exp2((scores - block_max) * factor)
        block_sum = jnp.sum(weights, axis=1, keepdims=True)
        block_acc = jnp.dot(
            weights.astype(jnp.bfloat16), v_buf[j], preferred_element_type=jnp.float32
        )
        new_max = jnp.maximum(run_max, block_max)
        old = jnp.exp2((run_max - new_max) * factor)
        new = jnp.exp2((block_max - new_max) * factor)
        return new_max, run_sum * old + block_sum * new, run_acc * old + block_acc * new

    start = (
        jnp.full((rows * heads, 1), neg_big, jnp.float32),
        jnp.zeros((rows * heads, 1), jnp.float32),
        jnp.zeros((rows * heads, HEAD_SIZE), jnp.float32),
    )
    carry = lax.fori_loop(0, block, lambda j, c: attend(j, c, False), start)
    _, total, acc = attend(block, carry, True)
    out = (acc / total).astype(o_ref.dtype)
    for n in range(heads):
        o_ref[0, :, n * HEAD_SIZE : (n + 1) * HEAD_SIZE] = out[n * rows : (n + 1) * rows]


def attention(query, locations, blocks, table):
    row_blocks, rows, width = query.shape
    count, span = len(blocks), blocks[0].shape[1]
    heads = width // HEAD_SIZE
    pairs = row_blocks * (row_blocks + 1) // 2 * rows * heads * span
    return pl.pallas_call(
        functools.partial(attention_kernel, count, heads),
        out_shape=jax.ShapeDtypeStruct(query.shape, jnp.bfloat16),
        grid_spec=pltpu.PrefetchScalarGridSpec(
            num_scalar_prefetch=1,
            grid=(row_blocks,),
            in_specs=[
                pl.BlockSpec((1, rows, 1), lambda b, t: (b, 0, 0)),
                pl.BlockSpec((1, rows, width), lambda b, t: (b, 0, 0)),
            ]
            + [pl.BlockSpec(memory_space=pl.ANY)] * count,
            out_specs=pl.BlockSpec((1, rows, width), lambda b, t: (b, 0, 0)),
            scratch_shapes=[
                pltpu.VMEM((count, span, HEAD_SIZE), jnp.bfloat16),
                pltpu.VMEM((count, span, HEAD_SIZE), jnp.bfloat16),
                pltpu.SemaphoreType.DMA((count, 2)),
            ],
        ),
        compiler_params=pltpu.CompilerParams(
            dimension_semantics=("arbitrary",), vmem_limit_bytes=40 << 20
        ),
        cost_estimate=pl.CostEstimate(
            flops=4 * pairs * HEAD_SIZE,
            bytes_accessed=4 * count * span * HEAD_SIZE + 4 * query.size,
            transcendentals=pairs,
        ),
    )(table, locations, query, *blocks)


def exit_kernel(steps, final, info, scale_ref, gain_ref, own_ref, other_ref, lex_ref, *rest):
    rest = list(rest)
    before = rest.pop(0)
    if final:
        div_ref, token_ref, out_ref, normed, acc, stats = rest
    else:
        acc, normed = rest
    tile, k = pl.program_id(0), pl.program_id(1)
    rows = own_ref.shape[1]
    width = lex_ref.shape[1]

    @pl.when(tile == 0)
    def _():
        gain = gain_ref[0]
        for n, ref in enumerate((own_ref, other_ref)):
            wide = ref[0].astype(jnp.float32)
            part = scale_ref[info[steps + n]]
            normed[k, n * rows : (n + 1) * rows] = (wide * part * gain).astype(jnp.bfloat16)

    product = jnp.dot(normed[k], lex_ref[...], preferred_element_type=jnp.float32)

    @pl.when(k == 0)
    def _():
        acc[...] = (before[...] + product) if before is not None else product

    @pl.when(k > 0)
    def _():
        acc[...] += product

    if final:

        @pl.when((tile == 0) & (k == 0))
        def _():
            lane = lax.broadcasted_iota(jnp.int32, stats.shape, 1)
            stats[...] = jnp.where(lane == 0, neg_big, 0.0)

        @pl.when(k == steps - 1)
        def _():
            for n in range(2):
                part = slice(n * rows, (n + 1) * rows)
                which = info[steps + n]
                scaled = acc[part] * (1.0 / div_ref[which])
                column = (
                    info[steps + 2]
                    + tile * width
                    + lax.broadcasted_iota(jnp.int32, scaled.shape, 1)
                )
                found = jnp.sum(
                    jnp.where(column == token_ref[which], scaled, 0.0), axis=1, keepdims=True
                )
                top, total, picked = stats[part, 0:1], stats[part, 1:2], stats[part, 2:3]
                new_top = jnp.maximum(top, jnp.max(scaled, axis=1, keepdims=True))
                total = total * jnp.exp(top - new_top) + jnp.sum(
                    jnp.exp(scaled - new_top), axis=1, keepdims=True
                )
                lane = lax.broadcasted_iota(jnp.int32, (rows, stats.shape[1]), 1)
                stats[part] = jnp.where(
                    lane == 0, new_top, jnp.where(lane == 1, total, picked + found)
                )

        @pl.when((k == steps - 1) & (tile == pl.num_programs(0) - 1))
        def _():
            out_ref[...] = stats[...]


def exit_piece(info, scale, gain, own, other, lexicon, before, row_args=None):
    steps, rows, depth = own.shape
    width = lexicon.shape[1]
    tile = min(1024, width)
    final = row_args is not None
    whole = lambda a: pl.BlockSpec(a.shape, lambda n, k, i: (0,) * a.ndim)
    piece = pl.BlockSpec((1, rows, depth), lambda n, k, i: (jnp.where(n == 0, k, steps - 1), 0, 0))
    wide = pl.BlockSpec((2 * rows, tile), lambda n, k, i: (0, n))
    in_specs = [
        whole(scale),
        pl.BlockSpec((1, 1, depth), lambda n, k, i: (i[k], 0, 0)),
        piece,
        piece,
        pl.BlockSpec((depth, tile), lambda n, k, i: (i[k], n)),
    ]
    args = [info, scale, gain, own, other, lexicon]
    body = functools.partial(exit_kernel, steps, final)
    if before is not None:
        in_specs.append(wide)
        args.append(before)
    else:
        inner = body
        body = lambda *refs: inner(*refs[:6], None, *refs[6:])
    normed = pltpu.VMEM((steps, 2 * rows, depth), jnp.bfloat16)
    if final:
        in_specs += [whole(a) for a in row_args]
        args += list(row_args)
        out_shape = jax.ShapeDtypeStruct((2 * rows, 128), jnp.float32)
        out_specs = pl.BlockSpec((2 * rows, 128), lambda n, k, i: (0, 0))
        scratch = [
            normed,
            pltpu.VMEM((2 * rows, tile), jnp.float32),
            pltpu.VMEM((2 * rows, 128), jnp.float32),
        ]
    else:
        out_shape = jax.ShapeDtypeStruct((2 * rows, width), jnp.float32)
        out_specs = wide
        scratch = [normed]
    return pl.pallas_call(
        body,
        out_shape=out_shape,
        grid_spec=pltpu.PrefetchScalarGridSpec(
            num_scalar_prefetch=1,
            grid=(width // tile, steps),
            in_specs=in_specs,
            out_specs=out_specs,
            scratch_shapes=scratch,
        ),
        compiler_params=pltpu.CompilerParams(
            dimension_semantics=("arbitrary", "arbitrary"), vmem_limit_bytes=48 << 20
        ),
        cost_estimate=pl.CostEstimate(
            flops=4 * steps * rows * depth * width,
            bytes_accessed=2 * steps * depth * (width + 2 * rows),
            transcendentals=0,
        ),
    )(*args)


def shards(
    moves,
    probe_vectors,
    lookup_tensor,
    payload_tensor,
    sequence_locations,
    attention_return_matrix,
    skip_stream_state,
    early_rescaling_factor,
    lexicon_projection_matrix,
    calibrating_divisor,
    desired_tokens_list,
):
    ctx, head = moves.ctx, moves.head
    i, h = lax.axis_index("ctx"), lax.axis_index("head")
    rows_here, width_here = probe_vectors.shape
    heads_here = width_here // HEAD_SIZE
    total_rows = rows_here * ctx
    kv_here = lookup_tensor.shape[1] // HEAD_SIZE
    half = ctx // kv_here
    head_parts = min(ctx, heads_here)
    row_parts = ctx // head_parts
    part_rows, part_width = rows_here // row_parts, width_here // head_parts

    mine = i // half

    def of_head(which):
        start = which * HEAD_SIZE
        return jnp.stack(
            [
                lax.dynamic_slice_in_dim(a, start, HEAD_SIZE, 1)
                for a in (lookup_tensor, payload_tensor)
            ]
        )

    kept = [(np.arange(ctx, dtype=np.int32), of_head(mine))]
    for shift in range(1, kv_here):
        sent = of_head((mine + shift) % kv_here)
        came = moves.ctx_move(sent, lambda s: (s + shift * half) % ctx)
        kept.append((np.array([(s - shift * half) % ctx for s in range(ctx)], np.int32), came))
    blocks, tables = [], []
    for n, (origin, block) in enumerate(kept):
        long, short = half // 2, half - 1 - half // 2
        ahead, behind = (long, short) if n % 2 == 0 else (short, long)
        for source, got in ring_gather(moves, block, half, ahead, behind):
            blocks.append(got)
            tables.append(origin[source])
    table = jnp.asarray(np.stack(tables, 1))[i]

    pieces = probe_vectors.reshape(row_parts, part_rows, head_parts, part_width)
    pieces = pieces.transpose(2, 0, 1, 3).reshape(ctx, part_rows, part_width)
    query = lax.all_to_all(pieces, "ctx", split_axis=0, concat_axis=0, tiled=True)
    locations = sequence_locations.reshape(ctx, row_parts, part_rows)
    locations = lax.dynamic_index_in_dim(locations, i % row_parts, 1, keepdims=False)
    attn = attention(query, locations[..., None], blocks, table)

    if row_parts == 1:
        mixed_part = None
        for source, got in ring_gather(
            moves, attn.reshape(total_rows, part_width), ctx, ctx // 2, ctx - 1 - ctx // 2
        ):
            start = jnp.asarray(source)[i] * part_width
            matrix = lax.dynamic_slice_in_dim(attention_return_matrix, start, part_width, 0)
            term = jnp.dot(got, matrix, preferred_element_type=jnp.float32)
            mixed_part = term if mixed_part is None else mixed_part + term
    else:
        every = lax.all_gather(attn, "ctx").reshape(
            head_parts, row_parts, ctx, part_rows, part_width
        )
        every = every.transpose(2, 1, 3, 0, 4).reshape(total_rows, width_here)
        mixed_part = jnp.dot(every, attention_return_matrix, preferred_element_type=jnp.float32)

    y, core = h // 2, h % 2
    depth = mixed_part.shape[1]
    exit_rows = total_rows // head
    quarters = mixed_part.reshape(head // 2, 2, exit_rows, depth)
    keep = lax.dynamic_index_in_dim(quarters, core, 1, keepdims=False)
    give = lax.dynamic_index_in_dim(quarters, 1 - core, 1, keepdims=False)
    both = keep + moves.core_swap(give)
    mixed_rows = lax.dynamic_index_in_dim(both, y, 0, keepdims=False) + moves.y_swap(
        lax.dynamic_index_in_dim(both, 1 - y, 0, keepdims=False)
    )
    hidden = (skip_stream_state.astype(jnp.float32) + mixed_rows).astype(jnp.bfloat16)

    widened = hidden.astype(jnp.float32)
    squares = jnp.zeros((head, exit_rows), jnp.float32)
    squares = lax.dynamic_update_slice(squares, jnp.sum(widened * widened, axis=1)[None], (h, 0))
    squares = butterfly(moves, squares, jnp.add)
    scale = lax.rsqrt(squares / (depth * ctx) + eps)[..., None]
    gain = lax.all_gather(early_rescaling_factor, "ctx").reshape(ctx, 1, depth)

    z = i // 2
    line, places = line_gather(moves, hidden, z)
    across = [moves.minor_swap(b) for b in line]
    beside = [moves.y_swap(b) for b in line]
    line, across, beside = (jnp.stack(b) for b in (line, across, beside))
    cut = exit_rows // 2
    diagonal = jnp.concatenate(
        [moves.y_swap(across[:, :cut]), moves.minor_swap(beside[:, cut:])], axis=1
    )

    vocab_here = lexicon_projection_matrix.shape[1]
    offset = (i * head + h) * vocab_here
    line_place = jnp.asarray(np.stack(places, 1))[z]
    row_args = (
        calibrating_divisor.reshape(head, exit_rows, 1),
        desired_tokens_list.reshape(head, exit_rows, 1),
    )

    def piece(stack, minor, y_of, before, args):
        rows_of = y_of * 2 + core
        info = jnp.concatenate(
            [line_place * 2 + minor, jnp.stack([rows_of, rows_of ^ 1, offset])]
        ).astype(jnp.int32)
        other = moves.core_swap(stack)
        return exit_piece(info, scale, gain, stack, other, lexicon_projection_matrix, before, args)

    minor = i % 2
    near = piece(line, minor, y, None, None)
    near = piece(across, 1 - minor, y, near, row_args)
    far = piece(beside, minor, 1 - y, None, None)
    far = piece(diagonal, 1 - minor, 1 - y, far, row_args)

    def in_order(pair, second):
        return jnp.where(second == 0, pair, pair[::-1])

    stats = jnp.stack([near, far])[:, :, :3].reshape(2, 2, exit_rows, 3)
    stats = in_order(stats, y)
    stats = jnp.where(core == 0, stats, stats[:, ::-1])
    stats = stats.reshape(total_rows, 3).T.reshape(3, total_rows)

    def merge(a, b):
        top = jnp.maximum(a[0], b[0])
        total = a[1] * jnp.exp(a[0] - top) + b[1] * jnp.exp(b[0] - top)
        return jnp.stack([top, total, a[2] + b[2]])

    peak, total, picked = butterfly(moves, stats, merge)
    return hidden, picked - peak - jnp.log(total)


def solution(mesh):
    placed = (
        P("ctx", "head"),
        P("ctx", "head"),
        P("ctx", "head"),
        P(),
        P("head", "ctx"),
        P("head", "ctx"),
        P("ctx"),
        P(None, ("ctx", "head")),
        P(),
        P(),
    )
    return jax.shard_map(
        functools.partial(shards, Moves(mesh)),
        mesh=mesh,
        in_specs=placed,
        out_specs=(P("head", "ctx"), P()),
        check_vma=False,
    )
```

```python
import functools
import math

import jax
import jax.numpy as jnp
import numpy as np
from jax import lax
from jax.experimental import pallas as pl
from jax.experimental.pallas import tpu as pltpu
from jax.sharding import PartitionSpec as P

HEAD_SIZE = 128

neg_big = -1e30
eps = 1e-05
AXES = ("ctx", "head")


class Moves:
    def __init__(self, mesh):
        self.ctx, self.head = mesh.shape["ctx"], mesh.shape["head"]

    def perm(self, ctx_to=None, head_to=None):
        pairs = []
        for i in range(self.ctx):
            for h in range(self.head):
                i2 = i if ctx_to is None else ctx_to(i)
                h2 = h if head_to is None else head_to(h)
                if i2 is not None and h2 is not None:
                    pairs.append((i * self.head + h, i2 * self.head + h2))
        return pairs

    def ctx_move(self, value, ctx_to):
        return lax.ppermute(value, AXES, self.perm(ctx_to=ctx_to))

    def head_move(self, value, head_to):
        return lax.ppermute(value, AXES, self.perm(head_to=head_to))

    def minor_swap(self, value):
        return self.ctx_move(value, lambda i: i ^ 1)

    def y_swap(self, value):
        return self.head_move(value, lambda h: h ^ 2)

    def core_swap(self, value):
        return self.head_move(value, lambda h: h ^ 1)


def ring_order(count):
    return list(range(0, count, 2)) + list(range(count - 1, 0, -2))


def ring_gather(moves, block, count, ahead, behind, halves=False):
    order = ring_order(count)
    place = {v: p for p, v in enumerate(order)}

    def shifted(i, step):
        base = i // count * count
        return base + order[(place[i - base] + step) % count]

    def source(step):
        return np.array([shifted(i, step) for i in range(moves.ctx)], np.int32)

    def forward_move(value):
        return moves.ctx_move(value, lambda i: shifted(i, 1))

    def backward_move(value):
        return moves.ctx_move(value, lambda i: shifted(i, -1))

    found = [(source(0), block)]
    forward = backward = block
    for k in range(1, max(ahead, behind) + 1):
        if k <= ahead:
            forward = forward_move(forward)
            found.append((source(-k), forward))
        if k <= behind:
            backward = backward_move(backward)
            found.append((source(k), backward))
    if halves:
        cut, k = block.shape[0] // 2, ahead + 1
        last = [forward_move(forward[:cut]), backward_move(backward[cut:])]
        found.append((source(k), jnp.concatenate(last)))
    return found


def square_gather(moves, kept, came):
    def origin(step):
        return np.arange(moves.ctx, dtype=np.int32) ^ step

    def move(value, step):
        return moves.ctx_move(value, lambda i: i ^ step)

    kept_z = move(kept, 2)
    kept_x = move(kept, 1)
    kept_xz = move(kept_z, 1)
    came_x = move(came, 1)
    came_z = move(came, 2)
    far = jnp.stack([move(came_x[0], 2), move(came_z[1], 1)])
    return (
        [(origin(0), kept), (origin(1), kept_x), (origin(2), kept_z), (origin(3), kept_xz)],
        [(origin(0), came), (origin(1), came_x), (origin(2), came_z), (origin(3), far)],
    )


def line_slots(length):
    arrivals = []
    for z in range(length):
        mine = []
        for k in range(1, length):
            pair = []
            if z + k < length:
                pair.append(("down", k, z + k))
            if z - k >= 0:
                pair.append(("up", k, z - k))
            if z >= length // 2:
                pair.reverse()
            mine += pair
        arrivals.append(mine)
    return [[arrivals[z][s] for z in range(length)] for s in range(length - 1)]


def line_gather(moves, block, z, arrived):
    length = moves.ctx // 2
    got = {("up", 0): block, ("down", 0): block}
    slots = line_slots(length)
    value, gate = block, arrived(0, block)
    for k in range(1, length):
        got["up", k] = moves.ctx_move(
            got["up", k - 1], lambda i: i + 2 if k - 1 <= i // 2 < length - 1 else None
        )
        got["down", k] = moves.ctx_move(
            got["down", k - 1], lambda i: i - 2 if 0 < i // 2 <= length - k else None
        )
        slot = slots[k - 1]
        choices = {}
        for place, (way, r, _) in enumerate(slot):
            choices.setdefault((way, r), []).append(place)
        options, *_ = lax.optimization_barrier(([got[key] for key in choices], value, gate))
        value = options[0]
        for option, where_z in list(zip(options, choices.values()))[1:]:
            here = functools.reduce(jnp.logical_or, [z == p for p in where_z])
            value = jnp.where(here, option, value)
        gate = arrived(k, value)


def ctx_butterfly(moves, value, merge):
    step = 1
    while step < moves.ctx:
        came = moves.ctx_move(value, lambda i: i ^ step)
        value = merge(value, came)
        step *= 2
    return value


def butterfly(moves, value, merge):
    step = 1
    while step < moves.head:
        value = merge(value, moves.head_move(value, lambda h: h ^ step))
        step *= 2
    return ctx_butterfly(moves, value, merge)


def attention_kernel(count, heads, table, loc_ref, q_ref, *rest):
    sources, (o_ref, k_buf, v_buf, sems) = rest[:count], rest[count:]
    block = pl.program_id(0)
    span = k_buf.shape[1]
    rows = q_ref.shape[1]
    factor = HEAD_SIZE ** (-0.5) * math.log2(math.e)

    @pl.when(block == 0)
    def _():
        copies = []
        for n, source in enumerate(sources):
            for part, buf in enumerate((k_buf, v_buf)):
                copies.append(
                    pltpu.make_async_copy(source.at[part], buf.at[table[n]], sems.at[n, part])
                )
        for copy in copies:
            copy.start()
        for copy in copies:
            copy.wait()

    query = jnp.concatenate(
        [q_ref[0, :, n * HEAD_SIZE : (n + 1) * HEAD_SIZE] for n in range(heads)], axis=0
    )

    def attend(j, carry, masked):
        run_max, run_sum, run_acc = carry
        scores = lax.dot_general(
            query, k_buf[j], (((1,), (1,)), ((), ())), preferred_element_type=jnp.float32
        )
        if masked:
            row_pos = jnp.concatenate([loc_ref[0]] * heads, axis=0)
            key_pos = j * span + lax.broadcasted_iota(jnp.int32, scores.shape, 1)
            scores = jnp.where(key_pos <= row_pos, scores, neg_big)
        block_max = jnp.max(scores, axis=1, keepdims=True)
        weights = jnp.exp2((scores - block_max) * factor)
        block_sum = jnp.sum(weights, axis=1, keepdims=True)
        block_acc = jnp.dot(
            weights.astype(jnp.bfloat16), v_buf[j], preferred_element_type=jnp.float32
        )
        new_max = jnp.maximum(run_max, block_max)
        old = jnp.exp2((run_max - new_max) * factor)
        new = jnp.exp2((block_max - new_max) * factor)
        return new_max, run_sum * old + block_sum * new, run_acc * old + block_acc * new

    start = (
        jnp.full((rows * heads, 1), neg_big, jnp.float32),
        jnp.zeros((rows * heads, 1), jnp.float32),
        jnp.zeros((rows * heads, HEAD_SIZE), jnp.float32),
    )
    carry = lax.fori_loop(0, block, lambda j, c: attend(j, c, False), start)
    _, total, acc = attend(block, carry, True)
    out = (acc / total).astype(o_ref.dtype)
    for n in range(heads):
        o_ref[0, :, n * HEAD_SIZE : (n + 1) * HEAD_SIZE] = out[n * rows : (n + 1) * rows]


def attention(query, locations, blocks, table):
    row_blocks, rows, width = query.shape
    count, span = len(blocks), blocks[0].shape[1]
    heads = width // HEAD_SIZE
    pairs = row_blocks * (row_blocks + 1) // 2 * rows * heads * span
    return pl.pallas_call(
        functools.partial(attention_kernel, count, heads),
        out_shape=jax.ShapeDtypeStruct(query.shape, jnp.bfloat16),
        grid_spec=pltpu.PrefetchScalarGridSpec(
            num_scalar_prefetch=1,
            grid=(row_blocks,),
            in_specs=[
                pl.BlockSpec((1, rows, 1), lambda b, t: (b, 0, 0)),
                pl.BlockSpec((1, rows, width), lambda b, t: (b, 0, 0)),
            ]
            + [pl.BlockSpec(memory_space=pl.ANY)] * count,
            out_specs=pl.BlockSpec((1, rows, width), lambda b, t: (b, 0, 0)),
            scratch_shapes=[
                pltpu.VMEM((count, span, HEAD_SIZE), jnp.bfloat16),
                pltpu.VMEM((count, span, HEAD_SIZE), jnp.bfloat16),
                pltpu.SemaphoreType.DMA((count, 2)),
            ],
        ),
        compiler_params=pltpu.CompilerParams(
            dimension_semantics=("arbitrary",), vmem_limit_bytes=40 << 20
        ),
        cost_estimate=pl.CostEstimate(
            flops=4 * pairs * HEAD_SIZE,
            bytes_accessed=4 * count * span * HEAD_SIZE + 4 * query.size,
            transcendentals=pairs,
        ),
    )(table, locations, query, *blocks)


def project_kernel(count, has_before, info, *refs):
    refs = list(refs)
    before = refs.pop(0) if has_before else None
    out = refs.pop()
    total = before[...] if has_before else None
    for n in range(count):
        term = jnp.dot(refs[n][...], refs[count + n][...], preferred_element_type=jnp.float32)
        total = term if total is None else total + term
    out[...] = total


def project(info, blocks, matrix, before, start, tiles, rows):
    count, depth = len(blocks), blocks[0].shape[1]
    width = matrix.shape[1]
    row_tile = pl.BlockSpec((rows, depth), lambda r, i: (i[start + r], 0))
    in_specs = [row_tile] * count
    for n in range(count):
        in_specs.append(pl.BlockSpec((depth, width), lambda r, i, n=n: (i[n], 0)))
    args = [*blocks] + [matrix] * count
    if before is not None:
        in_specs.insert(0, pl.BlockSpec((rows, width), lambda r, i: (i[start + r], 0)))
        args.insert(0, before)
    return pl.pallas_call(
        functools.partial(project_kernel, count, before is not None),
        out_shape=jax.ShapeDtypeStruct((tiles * rows, width), jnp.float32),
        grid_spec=pltpu.PrefetchScalarGridSpec(
            num_scalar_prefetch=1,
            grid=(tiles,),
            in_specs=in_specs,
            out_specs=pl.BlockSpec((rows, width), lambda r, i: (r, 0)),
        ),
        compiler_params=pltpu.CompilerParams(
            dimension_semantics=("arbitrary",), vmem_limit_bytes=40 << 20
        ),
        cost_estimate=pl.CostEstimate(
            flops=2 * tiles * rows * count * depth * width,
            bytes_accessed=2 * count * depth * (width + tiles * rows) + 4 * tiles * rows * width,
            transcendentals=0,
        ),
    )(info, *args)


def normalize_kernel(scale_ref, far_ref, gain_ref, *refs):
    parts, out_ref = refs[:-1], refs[-1]
    rows = parts[0].shape[0]
    for n, part in enumerate(parts):
        by = (scale_ref, far_ref)[n % 2][...]
        wide = part[...].astype(jnp.float32) * by * gain_ref[n // 2]
        out_ref[n // 2, n % 2 * rows : (n % 2 + 1) * rows] = wide.astype(out_ref.dtype)


def normalize(parts, scale, far_scale, gain):
    rows, depth = parts[0].shape
    return pl.pallas_call(
        normalize_kernel,
        out_shape=jax.ShapeDtypeStruct((2, 2 * rows, depth), jnp.bfloat16),
        compiler_params=pltpu.CompilerParams(vmem_limit_bytes=12 << 20),
        cost_estimate=pl.CostEstimate(
            flops=8 * rows * depth, bytes_accessed=16 * rows * depth, transcendentals=0
        ),
    )(scale, far_scale, gain[:, None, :], *parts)


def exit_kernel(final, has_before, info, own_ref, other_ref, *rest):
    rest = list(rest)
    steps, rows = own_ref.shape[:2]
    lex_refs, rest = rest[:steps], rest[steps:]
    before = rest.pop(0) if has_before else None
    part_width = lex_refs[0].shape[1] // 2
    tile, tiles = pl.program_id(0), pl.num_programs(0)

    def product(n, part):
        columns = slice(part * part_width, (part + 1) * part_width)
        total = before[n * rows : (n + 1) * rows, columns] if has_before else None
        ref = (own_ref, other_ref)[n]
        for k in range(steps):
            term = jnp.dot(ref[k], lex_refs[k][:, columns], preferred_element_type=jnp.float32)
            total = term if total is None else total + term
        return total

    if not final:
        (out_ref,) = rest
        for part in range(2):
            for n in range(2):
                out_ref[
                    n * rows : (n + 1) * rows, part * part_width : (part + 1) * part_width
                ] = product(n, part)
        return

    div_ref, token_ref, out_ref, first, second, tops, weights, picks = rest
    group = div_ref.shape[1]
    groups = 2 * rows // group
    inverse = [1.0 / div_ref[info[steps + g]] for g in range(groups)]

    @pl.when(tile == 0)
    def _():
        second[...] = jnp.full(second.shape, neg_big, jnp.float32)
        tops[...] = jnp.full(tops.shape, neg_big, jnp.float32)
        weights[...] = jnp.zeros(weights.shape, jnp.float32)
        picks[...] = jnp.zeros(picks.shape, jnp.float32)

    def count_in(ref, start, valid):
        for g in range(groups):
            part = slice(g * group, (g + 1) * group)
            value = ref[part]
            factor = inverse[g] * math.log2(math.e)
            token = token_ref[info[steps + g]] - start
            token = jnp.where(valid, token, -1)
            column = lax.broadcasted_iota(jnp.int32, value.shape, 1)
            found = jnp.sum(jnp.where(column == token, value, 0.0), axis=1, keepdims=True)
            top = tops[part]
            new_top = jnp.maximum(top, jnp.max(value, axis=1, keepdims=True))
            fresh = jnp.sum(jnp.exp2((value - new_top) * factor), axis=1, keepdims=True)
            weights[part] = weights[part] * jnp.exp2((top - new_top) * factor) + fresh
            tops[part] = new_top
            picks[part] += found

    start = info[steps + groups] + 2 * tile * part_width
    count_in(second, start - part_width, tile > 0)
    for n in range(2):
        first[n * rows : (n + 1) * rows] = product(n, 0)
    count_in(first, start, True)
    for n in range(2):
        second[n * rows : (n + 1) * rows] = product(n, 1)

    @pl.when(tile == tiles - 1)
    def _():
        count_in(second, start + part_width, True)
        for g in range(groups):
            part = slice(g * group, (g + 1) * group)
            lane = lax.broadcasted_iota(jnp.int32, (group, out_ref.shape[1]), 1)
            out_ref[part] = jnp.where(
                lane == 0,
                tops[part] * inverse[g],
                jnp.where(lane == 1, weights[part], picks[part] * inverse[g]),
            )


def exit_piece(info, own, other, lexicon, before, row_args):
    steps, rows, depth = own.shape
    width = lexicon.shape[1]
    tile = min(512, width)
    final = row_args is not None
    once = lambda a: pl.BlockSpec(
        a.shape, lambda n, i: (0,) * a.ndim, pipeline_mode=pl.Buffered(1)
    )
    wide = pl.BlockSpec((2 * rows, tile), lambda n, i: (0, n))
    in_specs = [once(own), once(other)]
    args = [info, own, other] + [lexicon] * steps
    for k in range(steps):
        in_specs.append(pl.BlockSpec((depth, tile), lambda n, i, k=k: (i[k], n)))
    if before is not None:
        in_specs.append(wide)
        args.append(pltpu.with_memory_space_constraint(before, pltpu.HBM))
    if final:
        in_specs += [once(a) for a in row_args]
        args += list(row_args)
        out_shape = jax.ShapeDtypeStruct((2 * rows, 128), jnp.float32)
        out_specs = pl.BlockSpec((2 * rows, 128), lambda n, i: (0, 0))
        scratch = [pltpu.VMEM((2 * rows, tile // 2), jnp.float32)] * 2
        scratch += [pltpu.VMEM((2 * rows, 1), jnp.float32)] * 3
    else:
        out_shape = pltpu.HBM((2 * rows, width), jnp.float32)
        out_specs = wide
        scratch = []
    return pl.pallas_call(
        functools.partial(exit_kernel, final, before is not None),
        out_shape=out_shape,
        grid_spec=pltpu.PrefetchScalarGridSpec(
            num_scalar_prefetch=1,
            grid=(width // tile,),
            in_specs=in_specs,
            out_specs=out_specs,
            scratch_shapes=scratch,
        ),
        compiler_params=pltpu.CompilerParams(
            dimension_semantics=("arbitrary",), vmem_limit_bytes=32 << 20
        ),
        cost_estimate=pl.CostEstimate(
            flops=4 * steps * rows * depth * width,
            bytes_accessed=2 * steps * depth * (width + 2 * rows),
            transcendentals=0,
        ),
    )(*args)


def shards(
    moves,
    probe_vectors,
    lookup_tensor,
    payload_tensor,
    sequence_locations,
    attention_return_matrix,
    skip_stream_state,
    early_rescaling_factor,
    lexicon_projection_matrix,
    calibrating_divisor,
    desired_tokens_list,
):
    return body(
        moves,
        probe_vectors,
        lookup_tensor,
        payload_tensor,
        sequence_locations,
        attention_return_matrix,
        skip_stream_state,
        early_rescaling_factor,
        lexicon_projection_matrix,
        calibrating_divisor,
        desired_tokens_list,
    )


def body(
    moves,
    probe_vectors,
    lookup_tensor,
    payload_tensor,
    sequence_locations,
    attention_return_matrix,
    skip_stream_state,
    early_rescaling_factor,
    lexicon_projection_matrix,
    calibrating_divisor,
    desired_tokens_list,
):
    ctx, head = moves.ctx, moves.head
    i, h = lax.axis_index("ctx"), lax.axis_index("head")
    rows_here, width_here = probe_vectors.shape
    heads_here = width_here // HEAD_SIZE
    total_rows = rows_here * ctx
    kv_here = lookup_tensor.shape[1] // HEAD_SIZE
    half = ctx // kv_here
    head_parts = min(ctx, heads_here)
    row_parts = ctx // head_parts
    part_rows, part_width = rows_here // row_parts, width_here // head_parts

    mine = i // half

    def of_head(which):
        start = which * HEAD_SIZE
        return jnp.stack(
            [
                lax.dynamic_slice_in_dim(a, start, HEAD_SIZE, 1)
                for a in (lookup_tensor, payload_tensor)
            ]
        )

    kept = [(np.arange(ctx, dtype=np.int32), of_head(mine))]
    for shift in range(1, kv_here):
        sent = of_head((mine + shift) % kv_here)
        came = moves.ctx_move(sent, lambda s: (s + shift * half) % ctx)
        kept.append((np.array([(s - shift * half) % ctx for s in range(ctx)], np.int32), came))
    blocks, tables = [], []
    squares = square_gather(moves, kept[0][1], kept[1][1]) if (half, kv_here) == (4, 2) else None
    for n, (origin, block) in enumerate(kept):
        if squares is not None:
            blocks += [got for _, got in squares[n]]
            tables += [origin[source] for source, _ in squares[n]]
            continue
        long, short = half // 2, half - 1 - half // 2
        ahead, behind = (long, short) if n % 2 == 0 else (short, long)
        for source, got in ring_gather(moves, block, half, ahead, behind):
            blocks.append(got)
            tables.append(origin[source])
    table = jnp.asarray(np.stack(tables, 1))[i]

    gain = early_rescaling_factor[None]
    step = 1
    while step < ctx:
        came = moves.ctx_move(gain, lambda n: n ^ step)
        gain = jnp.concatenate([gain, came])
        step *= 2
    slots = [[(None, 0, z) for z in range(ctx // 2)]] + line_slots(ctx // 2)
    vocab_here = lexicon_projection_matrix.shape[1]
    infos = np.zeros((ctx, head, len(slots), 7), np.int32)
    for a, b in np.ndindex(ctx, head):
        for n, slot in enumerate(slots):
            place = slot[a // 2][2] * 2
            infos[a, b, n, :2] = place + a % 2, place + 1 - a % 2
            infos[a, b, n, 2:] = b, b ^ 2, b ^ 1, b ^ 3, (a * head + b) * vocab_here
    infos = jnp.asarray(infos)[i, h]
    gains = jnp.take(gain, infos[:, :2] ^ i, axis=0, mode="clip")
    infos = [infos[n] for n in range(len(slots))]

    pieces = probe_vectors.reshape(row_parts, part_rows, head_parts, part_width)
    pieces = pieces.transpose(2, 0, 1, 3).reshape(ctx, part_rows, part_width)
    query = lax.all_to_all(pieces, "ctx", split_axis=0, concat_axis=0, tiled=True)
    locations = sequence_locations.reshape(ctx, row_parts, part_rows)
    locations = lax.dynamic_index_in_dim(locations, i % row_parts, 1, keepdims=False)
    locations, infos = lax.optimization_barrier((locations, infos))
    attn = attention(query, locations[..., None], blocks, table)

    y, core = h // 2, h % 2
    exit_rows = total_rows // head
    depth = attention_return_matrix.shape[1]
    tiles_of = np.array(
        [
            [(1 - n // 2) * 2 + 1 - n % 2, n // 2 * 2 + 1 - n % 2]
            + [(1 - n // 2) * 2 + n % 2, n // 2 * 2 + n % 2]
            for n in range(head)
        ],
        np.int32,
    )

    def table_of(sources, tiles):
        sources = np.broadcast_to(np.stack(sources, 1)[:, None], (ctx, head, len(sources)))
        tiles = np.broadcast_to(tiles[None], (ctx, head, tiles.shape[-1]))
        return jnp.asarray(np.concatenate([sources, tiles], 2).astype(np.int32))[i, h]

    if row_parts == 1:
        way = (ctx - 1) // 2
        ring = ring_gather(moves, attn.reshape(total_rows, part_width), ctx, way, way, halves=True)
        early, late = ring[:-1], ring[-1:]
        early_info = table_of([s for s, _ in early], np.tile(np.arange(head), (head, 1)))
        late_info = table_of([s for s, _ in late], tiles_of)
        early_sum = project(
            early_info,
            [b for _, b in early],
            attention_return_matrix,
            None,
            len(early),
            head,
            exit_rows,
        )

        def finish(first, tiles):
            return project(
                late_info,
                [b for _, b in late],
                attention_return_matrix,
                early_sum,
                len(late) + first,
                tiles,
                exit_rows,
            )
    else:
        every = lax.all_gather(attn, "ctx").reshape(
            head_parts, row_parts, ctx, part_rows, part_width
        )
        every = every.transpose(2, 1, 3, 0, 4).reshape(total_rows, width_here)
        late_info = table_of([np.zeros(ctx, np.int32)], tiles_of)

        def finish(first, tiles):
            return project(
                late_info, [every], attention_return_matrix, None, 1 + first, tiles, exit_rows
            )

    give = finish(0, 2)
    far_came = moves.core_swap(give[:exit_rows])
    near_came = moves.core_swap(give[exit_rows:])
    keep = finish(2, 2)
    far_sum = keep[:exit_rows] + far_came
    mixed_rows = (keep[exit_rows:] + near_came) + moves.y_swap(far_sum)
    hidden = (skip_stream_state.astype(jnp.float32) + mixed_rows).astype(jnp.bfloat16)

    length = ctx // 2
    widened = hidden.astype(jnp.float32)
    squares = jnp.sum(widened * widened, axis=1)
    step = 2
    while step < 2 * ctx:
        bit = step if step < ctx else 1
        squares = squares + moves.ctx_move(squares, lambda n: n ^ bit)
        step *= 2
    scale = lax.rsqrt(squares / (depth * ctx) + eps)[:, None]
    far_scale = moves.y_swap(scale)

    z = i // 2
    row_args = (
        calibrating_divisor.reshape(head, exit_rows, 1),
        desired_tokens_list.reshape(head, exit_rows, 1),
    )
    waiting, normed, logits = [], [], []

    def multiply():
        slot = len(logits)
        block, across, beside, far = waiting[slot]
        after = (logits[-1:], logits[-2:-1] + normed)[slot > 1 and slot < length - 1]
        parts, _ = lax.optimization_barrier(([block, beside, across, far], after))
        own = normalize(parts, scale, far_scale, gains[slot])
        other = moves.core_swap(own)
        logits.append(
            exit_piece(
                infos[slot],
                own,
                other,
                lexicon_projection_matrix,
                logits[-1] if logits else None,
                row_args if slot == length - 1 else None,
            )
        )
        normed[:] = [own]

    def arrived(slot, block):
        across = moves.minor_swap(block)
        beside = moves.y_swap(block)
        far = moves.y_swap(across) if slot % 2 == 0 else moves.minor_swap(beside)
        waiting.append((block, across, beside, far))
        if slot == length - 2:
            multiply()
        return logits

    line_gather(moves, hidden, z, arrived)
    while len(logits) < length:
        multiply()
    logits = logits[-1]

    def in_order(pair, second):
        return jnp.where(second == 0, pair, pair[::-1])

    stats = logits[:, :3].reshape(2, 2, exit_rows, 3).transpose(3, 1, 0, 2)
    stats = in_order(stats.transpose(1, 0, 2, 3), y)
    stats = in_order(stats.transpose(2, 1, 0, 3), core)
    stats = stats.transpose(1, 2, 0, 3).reshape(3, total_rows)

    def merge(a, b):
        top = jnp.maximum(a[0], b[0])
        total = a[1] * jnp.exp(a[0] - top) + b[1] * jnp.exp(b[0] - top)
        return jnp.stack([top, total, a[2] + b[2]])

    peak, total, picked = butterfly(moves, stats, merge)
    return hidden, picked - peak - jnp.log(total)


def solution(mesh):
    placed = (
        P("ctx", "head"),
        P("ctx", "head"),
        P("ctx", "head"),
        P(),
        P("head", "ctx"),
        P("head", "ctx"),
        P("ctx"),
        P(None, ("ctx", "head")),
        P(),
        P(),
    )
    return jax.shard_map(
        functools.partial(shards, Moves(mesh)),
        mesh=mesh,
        in_specs=placed,
        out_specs=(P("head", "ctx"), P()),
        check_vma=False,
    )
```

```python
import functools
import math

import jax
import jax.numpy as jnp
import numpy as np
from jax import lax
from jax.experimental import pallas as pl
from jax.experimental.pallas import tpu as pltpu
from jax.sharding import PartitionSpec as P

HEAD_SIZE = 128

neg_big = -1e30
eps = 1e-05
AXES = ("ctx", "head")


class Moves:
    def __init__(self, mesh):
        self.ctx, self.head = mesh.shape["ctx"], mesh.shape["head"]

    def perm(self, ctx_to=None, head_to=None):
        pairs = []
        for i in range(self.ctx):
            for h in range(self.head):
                i2 = i if ctx_to is None else ctx_to(i)
                h2 = h if head_to is None else head_to(h)
                if i2 is not None and h2 is not None:
                    pairs.append((i * self.head + h, i2 * self.head + h2))
        return pairs

    def ctx_move(self, value, ctx_to):
        return lax.ppermute(value, AXES, self.perm(ctx_to=ctx_to))

    def head_move(self, value, head_to):
        return lax.ppermute(value, AXES, self.perm(head_to=head_to))

    def minor_swap(self, value):
        return self.ctx_move(value, lambda i: i ^ 1)

    def y_swap(self, value):
        return self.head_move(value, lambda h: h ^ 2)

    def core_swap(self, value):
        return self.head_move(value, lambda h: h ^ 1)


def ring_order(count):
    return list(range(0, count, 2)) + list(range(count - 1, 0, -2))


def ring_gather(moves, block, count, ahead, behind, halves=False):
    order = ring_order(count)
    place = {v: p for p, v in enumerate(order)}

    def shifted(i, step):
        base = i // count * count
        return base + order[(place[i - base] + step) % count]

    def source(step):
        return np.array([shifted(i, step) for i in range(moves.ctx)], np.int32)

    def forward_move(value):
        return moves.ctx_move(value, lambda i: shifted(i, 1))

    def backward_move(value):
        return moves.ctx_move(value, lambda i: shifted(i, -1))

    found = [(source(0), block)]
    forward = backward = block
    for k in range(1, max(ahead, behind) + 1):
        if k <= ahead:
            forward = forward_move(forward)
            found.append((source(-k), forward))
        if k <= behind:
            backward = backward_move(backward)
            found.append((source(k), backward))
    if halves:
        cut, k = block.shape[0] // 2, ahead + 1
        last = [forward_move(forward[:cut]), backward_move(backward[cut:])]
        found.append((source(k), jnp.concatenate(last)))
    return found


def square_gather(moves, kept, came):
    def origin(step):
        return np.arange(moves.ctx, dtype=np.int32) ^ step

    def move(value, step):
        return moves.ctx_move(value, lambda i: i ^ step)

    kept_z = move(kept, 2)
    kept_x = move(kept, 1)
    kept_xz = move(kept_z, 1)
    came_x = move(came, 1)
    came_z = move(came, 2)
    far = move(came_x, 2)
    return (
        [(origin(0), kept), (origin(1), kept_x), (origin(2), kept_z), (origin(3), kept_xz)],
        [(origin(0), came), (origin(1), came_x), (origin(2), came_z), (origin(3), far)],
    )


def line_slots(length):
    arrivals = []
    for z in range(length):
        mine = []
        for k in range(1, length):
            pair = []
            if z + k < length:
                pair.append(("down", k, z + k))
            if z - k >= 0:
                pair.append(("up", k, z - k))
            if z >= length // 2:
                pair.reverse()
            mine += pair
        arrivals.append(mine)
    return [[arrivals[z][s] for z in range(length)] for s in range(length - 1)]


def line_gather(moves, block, z, arrived):
    length = moves.ctx // 2
    got = {("up", 0): block, ("down", 0): block}
    slots = line_slots(length)
    value, gate = block, arrived(0, block)
    for k in range(1, length):
        got["up", k] = moves.ctx_move(
            got["up", k - 1], lambda i: i + 2 if k - 1 <= i // 2 < length - 1 else None
        )
        got["down", k] = moves.ctx_move(
            got["down", k - 1], lambda i: i - 2 if 0 < i // 2 <= length - k else None
        )
        slot = slots[k - 1]
        choices = {}
        for place, (way, r, _) in enumerate(slot):
            choices.setdefault((way, r), []).append(place)
        options, *_ = lax.optimization_barrier(([got[key] for key in choices], value, gate))
        value = options[0]
        for option, where_z in list(zip(options, choices.values()))[1:]:
            here = functools.reduce(jnp.logical_or, [z == p for p in where_z])
            value = jnp.where(here, option, value)
        gate = arrived(k, value)


def ctx_butterfly(moves, value, merge):
    step = 1
    while step < moves.ctx:
        came = moves.ctx_move(value, lambda i: i ^ step)
        value = merge(value, came)
        step *= 2
    return value


def butterfly(moves, value, merge):
    step = 1
    while step < moves.head:
        value = merge(value, moves.head_move(value, lambda h: h ^ step))
        step *= 2
    return ctx_butterfly(moves, value, merge)


def attention_kernel(count, heads, table, loc_ref, q_ref, *rest):
    sources, (o_ref, k_buf, v_buf, sems) = rest[:count], rest[count:]
    block = pl.program_id(0)
    span = k_buf.shape[1]
    rows = q_ref.shape[1]
    factor = HEAD_SIZE ** (-0.5) * math.log2(math.e)

    @pl.when(block == 0)
    def _():
        copies = []
        for n, source in enumerate(sources):
            for part, buf in enumerate((k_buf, v_buf)):
                copies.append(
                    pltpu.make_async_copy(source.at[part], buf.at[table[n]], sems.at[n, part])
                )
        for copy in copies:
            copy.start()
        for copy in copies:
            copy.wait()

    query = jnp.concatenate(
        [q_ref[0, :, n * HEAD_SIZE : (n + 1) * HEAD_SIZE] for n in range(heads)], axis=0
    )

    def attend(j, carry, masked):
        run_max, run_sum, run_acc = carry
        scores = lax.dot_general(
            query, k_buf[j], (((1,), (1,)), ((), ())), preferred_element_type=jnp.float32
        )
        if masked:
            row_pos = jnp.concatenate([loc_ref[0]] * heads, axis=0)
            key_pos = j * span + lax.broadcasted_iota(jnp.int32, scores.shape, 1)
            scores = jnp.where(key_pos <= row_pos, scores, neg_big)
        block_max = jnp.max(scores, axis=1, keepdims=True)
        weights = jnp.exp2((scores - block_max) * factor)
        block_sum = jnp.sum(weights, axis=1, keepdims=True)
        block_acc = jnp.dot(
            weights.astype(jnp.bfloat16), v_buf[j], preferred_element_type=jnp.float32
        )
        new_max = jnp.maximum(run_max, block_max)
        old = jnp.exp2((run_max - new_max) * factor)
        new = jnp.exp2((block_max - new_max) * factor)
        return new_max, run_sum * old + block_sum * new, run_acc * old + block_acc * new

    start = (
        jnp.full((rows * heads, 1), neg_big, jnp.float32),
        jnp.zeros((rows * heads, 1), jnp.float32),
        jnp.zeros((rows * heads, HEAD_SIZE), jnp.float32),
    )
    carry = lax.fori_loop(0, block, lambda j, c: attend(j, c, False), start)
    _, total, acc = attend(block, carry, True)
    out = (acc / total).astype(o_ref.dtype)
    for n in range(heads):
        o_ref[0, :, n * HEAD_SIZE : (n + 1) * HEAD_SIZE] = out[n * rows : (n + 1) * rows]


def attention(query, locations, blocks, table):
    row_blocks, rows, width = query.shape
    count, span = len(blocks), blocks[0].shape[1]
    heads = width // HEAD_SIZE
    pairs = row_blocks * (row_blocks + 1) // 2 * rows * heads * span
    return pl.pallas_call(
        functools.partial(attention_kernel, count, heads),
        out_shape=jax.ShapeDtypeStruct(query.shape, jnp.bfloat16),
        grid_spec=pltpu.PrefetchScalarGridSpec(
            num_scalar_prefetch=1,
            grid=(row_blocks,),
            in_specs=[
                pl.BlockSpec((1, rows, 1), lambda b, t: (b, 0, 0)),
                pl.BlockSpec((1, rows, width), lambda b, t: (b, 0, 0)),
            ]
            + [pl.BlockSpec(memory_space=pl.ANY)] * count,
            out_specs=pl.BlockSpec((1, rows, width), lambda b, t: (b, 0, 0)),
            scratch_shapes=[
                pltpu.VMEM((count, span, HEAD_SIZE), jnp.bfloat16),
                pltpu.VMEM((count, span, HEAD_SIZE), jnp.bfloat16),
                pltpu.SemaphoreType.DMA((count, 2)),
            ],
        ),
        compiler_params=pltpu.CompilerParams(
            dimension_semantics=("arbitrary",), vmem_limit_bytes=40 << 20
        ),
        cost_estimate=pl.CostEstimate(
            flops=4 * pairs * HEAD_SIZE,
            bytes_accessed=4 * count * span * HEAD_SIZE + 4 * query.size,
            transcendentals=pairs,
        ),
    )(table, locations, query, *blocks)


def project_kernel(count, has_before, info, *refs):
    refs = list(refs)
    before = refs.pop(0) if has_before else None
    out = refs.pop()
    total = before[...] if has_before else None
    for n in range(count):
        term = jnp.dot(refs[n][...], refs[count + n][...], preferred_element_type=jnp.float32)
        total = term if total is None else total + term
    out[...] = total


def project(info, blocks, matrix, before, start, tiles, rows):
    count, depth = len(blocks), blocks[0].shape[1]
    width = matrix.shape[1]
    row_tile = pl.BlockSpec((rows, depth), lambda r, i: (i[start + r], 0))
    in_specs = [row_tile] * count
    for n in range(count):
        in_specs.append(pl.BlockSpec((depth, width), lambda r, i, n=n: (i[n], 0)))
    args = [*blocks] + [matrix] * count
    if before is not None:
        in_specs.insert(0, pl.BlockSpec((rows, width), lambda r, i: (i[start + r], 0)))
        args.insert(0, before)
    return pl.pallas_call(
        functools.partial(project_kernel, count, before is not None),
        out_shape=jax.ShapeDtypeStruct((tiles * rows, width), jnp.float32),
        grid_spec=pltpu.PrefetchScalarGridSpec(
            num_scalar_prefetch=1,
            grid=(tiles,),
            in_specs=in_specs,
            out_specs=pl.BlockSpec((rows, width), lambda r, i: (r, 0)),
        ),
        compiler_params=pltpu.CompilerParams(
            dimension_semantics=("arbitrary",), vmem_limit_bytes=40 << 20
        ),
        cost_estimate=pl.CostEstimate(
            flops=2 * tiles * rows * count * depth * width,
            bytes_accessed=2 * count * depth * (width + tiles * rows) + 4 * tiles * rows * width,
            transcendentals=0,
        ),
    )(info, *args)


def normalize_kernel(scale_ref, far_ref, gain_ref, *refs):
    parts, out_ref = refs[:-1], refs[-1]
    rows = parts[0].shape[0]
    for n, part in enumerate(parts):
        by = (scale_ref, far_ref)[n % 2][...]
        wide = part[...].astype(jnp.float32) * by * gain_ref[n // 2]
        out_ref[n // 2, n % 2 * rows : (n % 2 + 1) * rows] = wide.astype(out_ref.dtype)


def normalize(parts, scale, far_scale, gain):
    rows, depth = parts[0].shape
    return pl.pallas_call(
        normalize_kernel,
        out_shape=jax.ShapeDtypeStruct((2, 2 * rows, depth), jnp.bfloat16),
        compiler_params=pltpu.CompilerParams(vmem_limit_bytes=12 << 20),
        cost_estimate=pl.CostEstimate(
            flops=8 * rows * depth, bytes_accessed=16 * rows * depth, transcendentals=0
        ),
    )(scale, far_scale, gain[:, None, :], *parts)


def exit_kernel(final, has_before, info, own_ref, other_ref, *rest):
    rest = list(rest)
    steps, rows = own_ref.shape[:2]
    lex_refs, rest = rest[:steps], rest[steps:]
    before = rest.pop(0) if has_before else None
    part_width = lex_refs[0].shape[1] // 2
    tile, tiles = pl.program_id(0), pl.num_programs(0)

    def product(n, part):
        columns = slice(part * part_width, (part + 1) * part_width)
        total = before[n * rows : (n + 1) * rows, columns] if has_before else None
        ref = (own_ref, other_ref)[n]
        for k in range(steps):
            term = jnp.dot(ref[k], lex_refs[k][:, columns], preferred_element_type=jnp.float32)
            total = term if total is None else total + term
        return total

    if not final:
        (out_ref,) = rest
        for part in range(2):
            for n in range(2):
                out_ref[
                    n * rows : (n + 1) * rows, part * part_width : (part + 1) * part_width
                ] = product(n, part)
        return

    div_ref, token_ref, out_ref, first, second, tops, weights, picks = rest
    group = div_ref.shape[1]
    groups = 2 * rows // group
    inverse = [1.0 / div_ref[info[steps + g]] for g in range(groups)]

    @pl.when(tile == 0)
    def _():
        second[...] = jnp.full(second.shape, neg_big, jnp.float32)
        tops[...] = jnp.full(tops.shape, neg_big, jnp.float32)
        weights[...] = jnp.zeros(weights.shape, jnp.float32)
        picks[...] = jnp.zeros(picks.shape, jnp.float32)

    def count_in(ref, start, valid):
        for g in range(groups):
            part = slice(g * group, (g + 1) * group)
            value = ref[part]
            factor = inverse[g] * math.log2(math.e)
            token = token_ref[info[steps + g]] - start
            token = jnp.where(valid, token, -1)
            column = lax.broadcasted_iota(jnp.int32, value.shape, 1)
            found = jnp.sum(jnp.where(column == token, value, 0.0), axis=1, keepdims=True)
            top = tops[part]
            new_top = jnp.maximum(top, jnp.max(value, axis=1, keepdims=True))
            fresh = jnp.sum(jnp.exp2((value - new_top) * factor), axis=1, keepdims=True)
            weights[part] = weights[part] * jnp.exp2((top - new_top) * factor) + fresh
            tops[part] = new_top
            picks[part] += found

    start = info[steps + groups] + 2 * tile * part_width
    count_in(second, start - part_width, tile > 0)
    for n in range(2):
        first[n * rows : (n + 1) * rows] = product(n, 0)
    count_in(first, start, True)
    for n in range(2):
        second[n * rows : (n + 1) * rows] = product(n, 1)

    @pl.when(tile == tiles - 1)
    def _():
        count_in(second, start + part_width, True)
        for g in range(groups):
            part = slice(g * group, (g + 1) * group)
            lane = lax.broadcasted_iota(jnp.int32, (group, out_ref.shape[1]), 1)
            out_ref[part] = jnp.where(
                lane == 0,
                tops[part] * inverse[g],
                jnp.where(lane == 1, weights[part], picks[part] * inverse[g]),
            )


def exit_piece(info, own, other, lexicon, before, row_args):
    steps, rows, depth = own.shape
    width = lexicon.shape[1]
    tile = min(512, width)
    final = row_args is not None
    once = lambda a: pl.BlockSpec(
        a.shape, lambda n, i: (0,) * a.ndim, pipeline_mode=pl.Buffered(1)
    )
    wide = pl.BlockSpec((2 * rows, tile), lambda n, i: (0, n))
    in_specs = [once(own), once(other)]
    args = [info, own, other] + [lexicon] * steps
    for k in range(steps):
        in_specs.append(pl.BlockSpec((depth, tile), lambda n, i, k=k: (i[k], n)))
    if before is not None:
        in_specs.append(wide)
        args.append(pltpu.with_memory_space_constraint(before, pltpu.HBM))
    if final:
        in_specs += [once(a) for a in row_args]
        args += list(row_args)
        out_shape = jax.ShapeDtypeStruct((2 * rows, 128), jnp.float32)
        out_specs = pl.BlockSpec((2 * rows, 128), lambda n, i: (0, 0))
        scratch = [pltpu.VMEM((2 * rows, tile // 2), jnp.float32)] * 2
        scratch += [pltpu.VMEM((2 * rows, 1), jnp.float32)] * 3
    else:
        out_shape = pltpu.HBM((2 * rows, width), jnp.float32)
        out_specs = wide
        scratch = []
    return pl.pallas_call(
        functools.partial(exit_kernel, final, before is not None),
        out_shape=out_shape,
        grid_spec=pltpu.PrefetchScalarGridSpec(
            num_scalar_prefetch=1,
            grid=(width // tile,),
            in_specs=in_specs,
            out_specs=out_specs,
            scratch_shapes=scratch,
        ),
        compiler_params=pltpu.CompilerParams(
            dimension_semantics=("arbitrary",), vmem_limit_bytes=32 << 20
        ),
        cost_estimate=pl.CostEstimate(
            flops=4 * steps * rows * depth * width,
            bytes_accessed=2 * steps * depth * (width + 2 * rows),
            transcendentals=0,
        ),
    )(*args)


def shards(
    moves,
    probe_vectors,
    lookup_tensor,
    payload_tensor,
    sequence_locations,
    attention_return_matrix,
    skip_stream_state,
    early_rescaling_factor,
    lexicon_projection_matrix,
    calibrating_divisor,
    desired_tokens_list,
):
    return body(
        moves,
        probe_vectors,
        lookup_tensor,
        payload_tensor,
        sequence_locations,
        attention_return_matrix,
        skip_stream_state,
        early_rescaling_factor,
        lexicon_projection_matrix,
        calibrating_divisor,
        desired_tokens_list,
    )


def body(
    moves,
    probe_vectors,
    lookup_tensor,
    payload_tensor,
    sequence_locations,
    attention_return_matrix,
    skip_stream_state,
    early_rescaling_factor,
    lexicon_projection_matrix,
    calibrating_divisor,
    desired_tokens_list,
):
    ctx, head = moves.ctx, moves.head
    i, h = lax.axis_index("ctx"), lax.axis_index("head")
    rows_here, width_here = probe_vectors.shape
    heads_here = width_here // HEAD_SIZE
    total_rows = rows_here * ctx
    kv_here = lookup_tensor.shape[1] // HEAD_SIZE
    half = ctx // kv_here
    head_parts = min(ctx, heads_here)
    row_parts = ctx // head_parts
    part_rows, part_width = rows_here // row_parts, width_here // head_parts

    mine = i // half

    def of_head(which):
        start = which * HEAD_SIZE
        return jnp.stack(
            [
                lax.dynamic_slice_in_dim(a, start, HEAD_SIZE, 1)
                for a in (lookup_tensor, payload_tensor)
            ]
        )

    kept = [(np.arange(ctx, dtype=np.int32), of_head(mine))]
    for shift in range(1, kv_here):
        sent = of_head((mine + shift) % kv_here)
        came = moves.ctx_move(sent, lambda s: (s + shift * half) % ctx)
        kept.append((np.array([(s - shift * half) % ctx for s in range(ctx)], np.int32), came))
    blocks, tables = [], []
    squares = square_gather(moves, kept[0][1], kept[1][1]) if (half, kv_here) == (4, 2) else None
    for n, (origin, block) in enumerate(kept):
        if squares is not None:
            blocks += [got for _, got in squares[n]]
            tables += [origin[source] for source, _ in squares[n]]
            continue
        long, short = half // 2, half - 1 - half // 2
        ahead, behind = (long, short) if n % 2 == 0 else (short, long)
        for source, got in ring_gather(moves, block, half, ahead, behind):
            blocks.append(got)
            tables.append(origin[source])
    table = jnp.asarray(np.stack(tables, 1))[i]

    gain = early_rescaling_factor[None]
    step = 1
    while step < ctx:
        came = moves.ctx_move(gain, lambda n: n ^ step)
        gain = jnp.concatenate([gain, came])
        step *= 2
    slots = [[(None, 0, z) for z in range(ctx // 2)]] + line_slots(ctx // 2)
    vocab_here = lexicon_projection_matrix.shape[1]
    infos = np.zeros((ctx, head, len(slots), 7), np.int32)
    for a, b in np.ndindex(ctx, head):
        for n, slot in enumerate(slots):
            place = slot[a // 2][2] * 2
            infos[a, b, n, :2] = place + a % 2, place + 1 - a % 2
            infos[a, b, n, 2:] = b, b ^ 2, b ^ 1, b ^ 3, (a * head + b) * vocab_here
    infos = jnp.asarray(infos)[i, h]
    gains = jnp.take(gain, infos[:, :2] ^ i, axis=0, mode="clip")
    infos = [infos[n] for n in range(len(slots))]

    pieces = probe_vectors.reshape(row_parts, part_rows, head_parts, part_width)
    pieces = pieces.transpose(2, 0, 1, 3).reshape(ctx, part_rows, part_width)
    query = lax.all_to_all(pieces, "ctx", split_axis=0, concat_axis=0, tiled=True)
    locations = sequence_locations.reshape(ctx, row_parts, part_rows)
    locations = lax.dynamic_index_in_dim(locations, i % row_parts, 1, keepdims=False)
    locations, infos = lax.optimization_barrier((locations, infos))
    attn = attention(query, locations[..., None], blocks, table)

    y, core = h // 2, h % 2
    exit_rows = total_rows // head
    depth = attention_return_matrix.shape[1]
    tiles_of = np.array(
        [
            [(1 - n // 2) * 2 + 1 - n % 2, n // 2 * 2 + 1 - n % 2]
            + [(1 - n // 2) * 2 + n % 2, n // 2 * 2 + n % 2]
            for n in range(head)
        ],
        np.int32,
    )

    def table_of(sources, tiles):
        sources = np.broadcast_to(np.stack(sources, 1)[:, None], (ctx, head, len(sources)))
        tiles = np.broadcast_to(tiles[None], (ctx, head, tiles.shape[-1]))
        return jnp.asarray(np.concatenate([sources, tiles], 2).astype(np.int32))[i, h]

    if row_parts == 1:
        way = (ctx - 1) // 2
        ring = ring_gather(moves, attn.reshape(total_rows, part_width), ctx, way, way, halves=True)
        early, late = ring[:-1], ring[-1:]
        early_info = table_of([s for s, _ in early], np.tile(np.arange(head), (head, 1)))
        late_info = table_of([s for s, _ in late], tiles_of)
        early_sum = project(
            early_info,
            [b for _, b in early],
            attention_return_matrix,
            None,
            len(early),
            head,
            exit_rows,
        )

        def finish(first, tiles):
            return project(
                late_info,
                [b for _, b in late],
                attention_return_matrix,
                early_sum,
                len(late) + first,
                tiles,
                exit_rows,
            )
    else:
        every = lax.all_gather(attn, "ctx").reshape(
            head_parts, row_parts, ctx, part_rows, part_width
        )
        every = every.transpose(2, 1, 3, 0, 4).reshape(total_rows, width_here)
        late_info = table_of([np.zeros(ctx, np.int32)], tiles_of)

        def finish(first, tiles):
            return project(
                late_info, [every], attention_return_matrix, None, 1 + first, tiles, exit_rows
            )

    give = finish(0, 2)
    far_came = moves.core_swap(give[:exit_rows])
    near_came = moves.core_swap(give[exit_rows:])
    keep = finish(2, 2)
    far_sum = keep[:exit_rows] + far_came
    mixed_rows = (keep[exit_rows:] + near_came) + moves.y_swap(far_sum)
    hidden = (skip_stream_state.astype(jnp.float32) + mixed_rows).astype(jnp.bfloat16)

    length = ctx // 2
    widened = hidden.astype(jnp.float32)
    squares = jnp.sum(widened * widened, axis=1)
    step = 2
    while step < 2 * ctx:
        bit = step if step < ctx else 1
        squares = squares + moves.ctx_move(squares, lambda n: n ^ bit)
        step *= 2
    scale = lax.rsqrt(squares / (depth * ctx) + eps)[:, None]
    far_scale = moves.y_swap(scale)

    z = i // 2
    row_args = (
        calibrating_divisor.reshape(head, exit_rows, 1),
        desired_tokens_list.reshape(head, exit_rows, 1),
    )
    waiting, logits = [], []

    def multiply():
        slot = len(logits)
        block, across, beside, far = waiting[slot]
        after = (logits[-2:-1] if 1 < slot < length - 1 else logits[-1:]) or [waiting[-1][0]]
        parts, _ = lax.optimization_barrier(([block, beside, across, far], after))
        own = normalize(parts, scale, far_scale, gains[slot])
        other = moves.core_swap(own)
        logits.append(
            exit_piece(
                infos[slot],
                own,
                other,
                lexicon_projection_matrix,
                logits[-1] if logits else None,
                row_args if slot == length - 1 else None,
            )
        )

    def arrived(slot, block):
        across = moves.minor_swap(block)
        beside = moves.y_swap(block)
        far = moves.y_swap(across) if slot % 2 == 0 else moves.minor_swap(beside)
        waiting.append((block, across, beside, far))
        if slot == length - 2:
            multiply()
        return logits

    line_gather(moves, hidden, z, arrived)
    while len(logits) < length:
        multiply()
    logits = logits[-1]

    def in_order(pair, second):
        return jnp.where(second == 0, pair, pair[::-1])

    stats = logits[:, :3].reshape(2, 2, exit_rows, 3).transpose(3, 1, 0, 2)
    stats = in_order(stats.transpose(1, 0, 2, 3), y)
    stats = in_order(stats.transpose(2, 1, 0, 3), core)
    stats = stats.transpose(1, 2, 0, 3).reshape(3, total_rows)

    def merge(a, b):
        top = jnp.maximum(a[0], b[0])
        total = a[1] * jnp.exp(a[0] - top) + b[1] * jnp.exp(b[0] - top)
        return jnp.stack([top, total, a[2] + b[2]])

    peak, total, picked = butterfly(moves, stats, merge)
    return hidden, picked - peak - jnp.log(total)


def solution(mesh):
    placed = (
        P("ctx", "head"),
        P("ctx", "head"),
        P("ctx", "head"),
        P(),
        P("head", "ctx"),
        P("head", "ctx"),
        P("ctx"),
        P(None, ("ctx", "head")),
        P(),
        P(),
    )
    return jax.shard_map(
        functools.partial(shards, Moves(mesh)),
        mesh=mesh,
        in_specs=placed,
        out_specs=(P("head", "ctx"), P()),
        check_vma=False,
    )
```
